512 devices in a mesh: blk: 128 (over z, x, core), rhs: 4 (over y).
Axes of the slice: x: 4, y: 4, z: 16, core: 2. Of those that a mesh axis runs over, the one named last changes fastest.
Arguments:
- right_sides: bfloat16 [4, 4, 128, 320, 256], P(None, None, 'blk', 'rhs'), may hold values from -6 to 6
- inverse_blocks: bfloat16 [4, 4, 128, 256, 256], P(None, None, 'blk', 'rhs'), as said below
- lower_blocks: bfloat16 [3, 4, 128, 6, 256, 256], P(None, None, 'blk', None, 'rhs'), may hold values from -0.21875 to 0.21875
- row_counts: int32 [3, 4, 128], P(None, None, 'blk'), may hold values from 1 to 6, as said below
Outputs:
- solution: bfloat16 [4, 4, 128, 320, 256], P(None, None, 'blk', 'rhs')
The draws below stay inside these ranges and needn't reach their ends.
Inputs may be any that keep to these rules, and one draw needn't show every extreme that they name: `row_counts`: in every level some supernode column has 6 row blocks. Every block of inverse_blocks is lower triangular: its entries above the diagonal are zero and its diagonal entries are positive.
All inputs are finite; a program needn't handle non-finite values.
Results may differ from the reference program's by a relative error of at most 0.0061.
Values may be sent and summed in bfloat16 or wider, within the bound.
No kernel may reach another device: no remote copies, remote signals or barrier semaphores. Data moves between devices by JAX's collectives and lax.ppermute only.
A program may use at most 64 MiB of HBM per device.

```python
import math
import jax
import jax.numpy as jnp
from jax import lax

BLOCK = 256
COLS_DEV = 4
LEVELS = 4
REACH = 6
OWNERS = 128
RHS = 320


def draw_row_counts(key, part):
    total = COLS_DEV * OWNERS
    base_counts = jax.random.randint(jax.random.fold_in(key, 11), (LEVELS - 1, total), 1, 4)
    heavy_counts = jax.random.randint(jax.random.fold_in(key, 13), (LEVELS - 1, total), 4, REACH + 1)
    heavy_pick = jax.random.randint(jax.random.fold_in(key, 14), (LEVELS - 1, total), 0, 16)
    counts = jnp.where(heavy_pick == 0, heavy_counts, base_counts)
    peak_index = jax.random.randint(jax.random.fold_in(key, 12), (LEVELS - 1, 1), 0, total)
    column_index = lax.broadcasted_iota(jnp.int32, (LEVELS - 1, total), 1)
    counts = jnp.where(column_index == peak_index, REACH, counts)
    return counts.reshape(LEVELS - 1, COLS_DEV, OWNERS).astype(jnp.int32)


def draw_inverse_blocks(key, part):
    shape = (LEVELS, COLS_DEV, OWNERS, BLOCK, BLOCK)
    row_index = lax.broadcasted_iota(jnp.int32, shape, 3)
    column_index = lax.broadcasted_iota(jnp.int32, shape, 4)
    lower_part = jax.random.normal(jax.random.fold_in(key, 21), shape, jnp.float32)
    lower_part = lower_part * (0.8 / math.sqrt(BLOCK))
    diagonal_part = jax.random.uniform(jax.random.fold_in(key, 22), shape[:4], jnp.float32, 0.6, 1.4)
    matrix = jnp.where(column_index < row_index, lower_part, 0.0)
    matrix = matrix + jnp.where(column_index == row_index, diagonal_part[..., None], 0.0)
    return matrix.astype(jnp.bfloat16)


def shard_levels(key, extent, split, smallest, largest):
    gain, own = 1.0, jax.random.fold_in(key, 6)
    for dim, parts in split:
        steps = jnp.exp(jax.random.uniform(jax.random.fold_in(own, dim), (parts,), jnp.float32, smallest / len(split), largest / len(split)))
        gain = gain * jnp.repeat(steps, extent[dim] // parts).reshape([-1 if axis == dim else 1 for axis in range(len(extent))])
    return gain


def bell_draw(own_key, extent, width, limit, cuts=(), kind=jnp.bfloat16):
    values = jax.random.normal(own_key, extent, jnp.float32) * width
    if len(cuts) > 0:
        values = shard_levels(own_key, extent, cuts, -0.22, 0.18) * values
    return jnp.clip(values, min=-limit, max=limit).astype(kind)


def setup_inputs(seed: int = 0) -> dict:
    arg_keys = jax.random.split(jax.random.key(seed), 5)
    right_sides = bell_draw(arg_keys[0], (LEVELS, COLS_DEV, OWNERS, RHS, BLOCK), 1.0, 6.0, ((2, 128), (3, 4)))
    inverse_blocks = draw_inverse_blocks(jax.random.fold_in(arg_keys[4], 71), 0)
    lower_blocks = bell_draw(arg_keys[2], (LEVELS - 1, COLS_DEV, OWNERS, REACH, BLOCK, BLOCK), (3 * BLOCK) ** -0.5, 0.21875, ((2, 128), (4, 4)))
    row_counts = draw_row_counts(jax.random.fold_in(arg_keys[4], 71), 0)
    return {"right_sides": right_sides, "inverse_blocks": inverse_blocks, "lower_blocks": lower_blocks, "row_counts": row_counts}


def slot_offset(slot):
    return (slot // 2 + 1) * (1 if slot % 2 == 0 else -1)


def reference(right_sides, inverse_blocks, lower_blocks, row_counts):
    incoming = jnp.zeros((COLS_DEV, OWNERS, RHS, BLOCK), jnp.float32)
    solved_levels = []
    for level in range(LEVELS):
        rest_block = (right_sides[level].astype(jnp.float32) - incoming).astype(jnp.bfloat16)
        solved = jnp.einsum("kprj,kpij->kpri", rest_block.astype(jnp.float32),
                            inverse_blocks[level].astype(jnp.float32)).astype(jnp.bfloat16)
        solved_levels.append(solved)
        if level + 1 < LEVELS:
            incoming = jnp.zeros((COLS_DEV, OWNERS, RHS, BLOCK), jnp.float32)
            solved_wide = solved.astype(jnp.float32)
            for slot in range(REACH):
                updates = jnp.einsum("kpij,kprj->kpri", lower_blocks[level, :, :, slot].astype(jnp.float32), solved_wide)
                active = (row_counts[level] > slot).astype(jnp.float32)[:, :, None, None]
                incoming = incoming + jnp.roll(updates * active, slot_offset(slot), axis=1)
    return jnp.stack(solved_levels)
```

```python
import jax
import jax.numpy as jnp
from jax import lax
from jax.sharding import PartitionSpec as P

AXES = ("blk", "rhs")
BATCHES = ((0,), (1,), (2, 3))


def local(n_blk, right_sides, inverse_blocks, lower_blocks, row_counts):
    levels = right_sides.shape[0]
    chunk, block = inverse_blocks.shape[3], inverse_blocks.shape[4]
    part = right_sides.shape[3]
    core = lax.axis_index("blk") % 2
    me = lax.axis_index("rhs")
    first = jnp.where(core == 0, 1, 3)
    second = 4 - first
    bf16, f32 = jnp.bfloat16, jnp.float32

    def routed(x, to):
        pairs = []
        for b in range(n_blk):
            for r in range(4):
                nb, nr = to(b, r)
                pairs.append((b * 4 + r, (nb % n_blk) * 4 + nr))
        return lax.ppermute(x, AXES, pairs)

    def to_first(x):
        return routed(x, lambda b, r: (b, r ^ (1 if b % 2 == 0 else 3)))

    def to_second(x):
        return routed(x, lambda b, r: (b, r ^ (3 if b % 2 == 0 else 1)))

    def to_core(x):
        return routed(x, lambda b, r: (b ^ 1, r))

    def to_next(x, chips):
        return routed(x, lambda b, r: (b + 2 * chips if b % 2 == 0 else b - 2 * chips, r))

    def exchanged(pick):
        got1 = to_first(jnp.stack([pick(first), pick(2)]))
        got2 = to_second(jnp.stack([pick(second), got1[1]]))
        one = jnp.where(core == 0, got1[0], got2[0])
        three = jnp.where(core == 0, got2[0], got1[0])
        return jnp.stack([pick(0), one, got2[1], three])

    def in_order(x):
        x = jnp.where(me & 1, jnp.stack([x[1], x[0], x[3], x[2]]), x)
        return jnp.where(me & 2, jnp.concatenate([x[2:], x[:2]]), x)

    def dyn(x, i, axis):
        return lax.dynamic_index_in_dim(x, i, axis, keepdims=False)

    lower = lower_blocks[:, :, 0]
    slot = jnp.arange(lower.shape[2], dtype=jnp.int32)
    active = slot[None, None, :] < row_counts
    lower = jnp.where(active[..., None, None], lower, jnp.zeros((), bf16))
    lower = lower.reshape(lower.shape[:2] + (3, 2, chunk, block))

    def rows_of(level, e):
        k = me ^ e
        rows = [dyn(inverse_blocks[level, :, 0], k, 0), dyn(right_sides[level, :, 0], k, 0)]
        if level + 1 < levels:
            mine = dyn(lower[level], k, 0)
            rows.append(dyn(mine, core, 1).reshape(3 * chunk, block))
            rows.append(dyn(mine, 1 - core, 1).reshape(3 * chunk, block))
        return rows

    data = {}
    for batch in BATCHES:
        got = exchanged(lambda e: jnp.concatenate(sum([rows_of(level, e) for level in batch], [])))
        at = 0
        own, send = [], []
        for level in batch:
            inv = in_order(got[:, at : at + chunk]).reshape(block, block)
            at += chunk
            right = got[:, at : at + part].reshape(4 * part, block)
            at += part
            pieces = [inv, right]
            if level + 1 < levels:
                for _ in range(2):
                    low = in_order(got[:, at : at + 3 * chunk]).reshape(4, 3, chunk, block)
                    pieces.append(low.transpose(1, 0, 2, 3).reshape(3 * block, block))
                    at += 3 * chunk
                send += [inv, right, pieces[3]]
            else:
                send += [inv, right]
            own.append(pieces)
        other = to_core(jnp.concatenate(send))
        at = 0
        for level, pieces in zip(batch, own):
            inv = jnp.stack([pieces[0], other[at : at + block]])
            at += block
            right = jnp.stack([pieces[1], other[at : at + 4 * part]])
            at += 4 * part
            low = None
            if level + 1 < levels:
                low = jnp.stack([pieces[2], other[at : at + 3 * block]]).reshape(2, 3, block, block)
                at += 3 * block
            data[level] = (inv, right, low)

    incoming = None
    solved_levels = []
    for level in range(levels):
        inv, right, low = data[level]
        rest = right if incoming is None else (right.astype(f32) - incoming).astype(bf16)
        solved = jnp.einsum("prj,pij->pri", rest, inv, preferred_element_type=f32).astype(bf16)
        solved_levels.append(solved[0])
        if level + 1 < levels:
            updates = jnp.einsum("prj,pmij->pmri", solved, low, preferred_element_type=f32)
            far = to_next(updates[1, 2].astype(bf16), 2)
            near = jnp.stack([updates[0, 1] + updates[1, 0], updates[0, 2] + updates[1, 1]])
            near = to_next(near.astype(bf16), 1).astype(f32)
            mine = jnp.stack([near[0] + far.astype(f32), near[1] + updates[0, 0]]).astype(bf16)
            theirs = to_core(mine)
            incoming = mine.astype(f32) + theirs[::-1].astype(f32)

    out = jnp.stack(solved_levels).reshape(levels, 4, part, block)
    out = exchanged(lambda e: dyn(out, jnp.asarray(e), 1))
    return in_order(out).transpose(1, 0, 2, 3)[:, :, None]


def solution(mesh):
    n_blk = mesh.shape["blk"]
    return jax.shard_map(
        lambda *args: local(n_blk, *args),
        mesh=mesh,
        in_specs=(
            P(None, None, "blk", "rhs", None),
            P(None, None, "blk", "rhs", None),
            P(None, None, "blk", None, "rhs", None),
            P(None, None, "blk"),
        ),
        out_specs=P(None, None, "blk", "rhs", None),
        check_vma=False,
    )
```
